256 devices in a mesh: seq: 16 (over x, y), resp: 16 (over z, core).
Axes of the slice: x: 4, y: 4, z: 8, core: 2. Of those that a mesh axis runs over, the one named last changes fastest.
Arguments:
- queries: bfloat16 [16, 8192, 1024], P('resp', 'seq'), may hold values from -1.796875 to 1.796875
- keys: bfloat16 [16, 8192, 1024], P('resp', 'seq'), may hold values from -1.796875 to 1.796875
- values: bfloat16 [16, 8192, 1024], P('resp', 'seq'), may hold values from -6 to 6
- grad_out: bfloat16 [16, 8192, 1024], P('resp', 'seq'), may hold values from -6 to 6
- lengths: int32 [15], replicated, may hold values from 8 to 16
Outputs:
- attended: bfloat16 [16, 8192, 1024], P('resp', 'seq')
- grad_queries: bfloat16 [16, 8192, 1024], P('resp', 'seq')
- grad_keys: bfloat16 [16, 8192, 1024], P('resp', 'seq')
- grad_values: bfloat16 [16, 8192, 1024], P('resp', 'seq')
The draws below stay inside these ranges and needn't reach their ends.
All inputs are finite; a program needn't handle non-finite values.
Results may differ from the reference program's by a relative error of at most 0.005.
Values sent between devices are 32-bit elements; how exact they have to be, the bound alone decides.
A program may use at most 128 MiB of HBM per device.

```python
import math
import jax
import jax.numpy as jnp
from jax import lax

HEADS = 8
HEAD = 128
BLOCK = 512
ROW_TOKENS = 8192
ROWS = 16
RESP_BLOCKS = 16


def touch_ends(drawn, rng, low, top_value):
    spot = [jax.random.randint(jax.random.fold_in(rng, axis), (), 0, length) for axis, length in enumerate(drawn.shape)]
    longest = drawn.shape.index(max(drawn.shape))
    neighbour = spot[:longest] + [(spot[longest] + 1) % drawn.shape[longest]] + spot[longest + 1:]
    return drawn.at[tuple(spot)].set(low).at[tuple(neighbour)].set(top_value)


def steps_of(rng, extent, pieces, low, largest):
    def one(position, parts):
        steps = jax.random.uniform(jax.random.fold_in(jax.random.fold_in(rng, 6), position), (parts,), jnp.float32, low / len(pieces), largest / len(pieces))
        return jnp.repeat(jnp.exp(steps), extent[position] // parts).reshape((-1,) + (1,) * (len(extent) - position - 1))

    level = one(*pieces[0])
    for cut in pieces[1:]:
        level = level * one(*cut)
    return level


def scatter_about(own_key, shape, scale, reach, pieces=(), held_as=jnp.bfloat16):
    entries = scale * jax.random.normal(own_key, shape, jnp.float32)
    if pieces:
        entries = entries * steps_of(own_key, shape, pieces, -0.22, 0.18)
    return jnp.clip(entries, -reach, reach).astype(held_as)


def setup_inputs(seed: int = 0) -> dict:
    key_of = jax.random.split(jax.random.key(seed), 6)
    return {
        "queries": scatter_about(key_of[0], (ROWS, ROW_TOKENS, HEADS * HEAD), 0.3, 1.796875, ((0, 16), (1, 16))),
        "keys": scatter_about(key_of[1], (ROWS, ROW_TOKENS, HEADS * HEAD), 0.3, 1.796875, ((0, 16), (1, 16))),
        "values": scatter_about(key_of[2], (ROWS, ROW_TOKENS, HEADS * HEAD), 1.0, 6.0, ((0, 16), (1, 16))),
        "grad_out": scatter_about(key_of[3], (ROWS, ROW_TOKENS, HEADS * HEAD), 1.0, 6.0, ((0, 16), (1, 16))),
        "lengths": touch_ends(jax.random.randint(key_of[4], (ROWS - 1,), RESP_BLOCKS // 2, RESP_BLOCKS + 1), jax.random.fold_in(key_of[4], 1), RESP_BLOCKS // 2, RESP_BLOCKS).astype(jnp.int32),
    }


def lower_round(array):
    narrow = lax.optimization_barrier(array.astype(jnp.bfloat16))
    return narrow.astype(jnp.float32)

def block_pass(query_block, key_block, value_block, grad_block, forward_state, backward_state, factor):
    block_rows = query_block.shape[0]
    causal = (jnp.arange(block_rows)[:, None] >= jnp.arange(block_rows)[None, :])[None]
    query_wide = query_block.astype(jnp.float32)
    key_wide = key_block.astype(jnp.float32)
    value_wide = value_block.astype(jnp.float32)
    grad_wide = grad_block.astype(jnp.float32)
    attend = lower_round(jnp.where(causal, jnp.einsum('thd,shd->hts', query_wide, key_wide) * factor, 0.0))
    pushed = lower_round(jnp.where(causal, jnp.einsum('thd,shd->hts', grad_wide, value_wide) * factor, 0.0))
    forward_low = lower_round(forward_state)
    backward_low = lower_round(backward_state)
    attended = jnp.einsum('hts,shd->thd', attend, value_wide) + factor * jnp.einsum('thi,hij->thj', query_wide, forward_low)
    grad_query = jnp.einsum('hts,shi->thi', pushed, key_wide) + factor * jnp.einsum('thj,hij->thi', grad_wide, forward_low)
    grad_key = jnp.einsum('hts,thi->shi', pushed, query_wide) + factor * jnp.einsum('shj,hij->shi', value_wide, backward_low)
    grad_value = jnp.einsum('hts,thi->shi', attend, grad_wide) + factor * jnp.einsum('shi,hij->shj', key_wide, backward_low)
    return (attended.astype(jnp.bfloat16), grad_query.astype(jnp.bfloat16), grad_key.astype(jnp.bfloat16), grad_value.astype(jnp.bfloat16))

def reference(queries, keys, values, grad_out, lengths):
    row_count = queries.shape[0]
    length = queries.shape[1]
    row_width = queries.shape[2]
    factor = 1.0 / math.sqrt(2.0 * length)
    limits = jnp.concatenate([jnp.array([length], dtype=jnp.int32), (lengths * BLOCK).astype(jnp.int32)])
    keep_mask = (jnp.arange(length, dtype=jnp.int32)[None, :] < limits[:, None]).astype(jnp.bfloat16)[:, :, None]
    masked = tuple(((array * keep_mask).reshape(row_count, length, HEADS, HEAD) for array in (queries, keys, values, grad_out)))

    def totals(arrays):
        query_row, key_row, value_row, grad_row = arrays
        state_kv = jnp.einsum('thi,thj->hij', key_row.astype(jnp.float32), value_row.astype(jnp.float32))
        state_qg = jnp.einsum('thi,thj->hij', query_row.astype(jnp.float32), grad_row.astype(jnp.float32))
        return (state_kv, state_qg)
    kv_rows, qg_rows = lax.map(totals, masked)
    prompt_state = kv_rows[0]
    answer_state = lax.optimization_barrier(jnp.sum(qg_rows[1:], axis=0))
    blocks = length // BLOCK

    def one_row(arrays):
        row_index = arrays[0]
        shaped = tuple((array.reshape(blocks, BLOCK, HEADS, HEAD) for array in arrays[1:]))
        kv_blocks = jnp.einsum('bthi,bthj->bhij', shaped[1].astype(jnp.float32), shaped[2].astype(jnp.float32))
        qg_blocks = jnp.einsum('bthi,bthj->bhij', shaped[0].astype(jnp.float32), shaped[3].astype(jnp.float32))
        start_state = jnp.where(row_index == 0, jnp.zeros_like(prompt_state), prompt_state)
        end_state = jnp.where(row_index == 0, answer_state, jnp.zeros_like(answer_state))
        forward = start_state[None] + jnp.cumsum(kv_blocks, axis=0) - kv_blocks
        backward = end_state[None] + (lax.optimization_barrier(jnp.sum(qg_blocks, axis=0))[None] - jnp.cumsum(qg_blocks, axis=0))
        results = lax.map(lambda items: block_pass(items[0], items[1], items[2], items[3], items[4], items[5], factor), (shaped[0], shaped[1], shaped[2], shaped[3], forward, backward))
        return tuple((result.reshape(length, row_width) for result in results))
    outputs = lax.map(one_row, (jnp.arange(row_count, dtype=jnp.int32), masked[0], masked[1], masked[2], masked[3]))
    return (outputs[0], outputs[1], outputs[2], outputs[3])
```

```python
import math

import jax
import jax.numpy as jnp
from jax import lax
from jax.experimental import pallas as pl
from jax.experimental.pallas import tpu as pltpu
from jax.sharding import PartitionSpec as P

HEADS = 8
HEAD = 128
BLOCK = 512
HALF = 256
SEQ = 16
RESP = 16
SHARD = HEADS * HEAD // SEQ
MESH = pl.DeviceIdType.MESH
FACTOR = 1.0 / math.sqrt(2.0 * SEQ * BLOCK)


def dot(a, b, dims):
    return lax.dot_general(a, b, (dims, ((), ())), preferred_element_type=jnp.float32)


NN = ((1,), (0,))
NT = ((1,), (1,))
TN = ((0,), (0,))


def kernel(
    len_ref, k_hbm, v_hbm, q_hbm, g_hbm,
    att_ref, gq_ref, gv_ref, gk_ref,
    x, st, rc, rt, fin, zs, zr, intra,
    in_sem, s1, r1, s2, r2, sz, rz,
):
    me = lax.axis_index("seq")
    row = lax.axis_index("resp")
    fst = (row + RESP - 2) // (RESP - 1)
    snd = 1 - fst

    barrier = pltpu.get_barrier_semaphore()

    def greet(i, _):
        pl.semaphore_signal(barrier, inc=1, device_id=((me + i) % SEQ, row), device_id_type=MESH)
        return 0

    lax.fori_loop(1, SEQ, greet, 0)

    def greet_row(i, _):
        pl.semaphore_signal(barrier, inc=1, device_id=(me, i), device_id_type=MESH)
        return 0

    @pl.when(row == 0)
    def _():
        lax.fori_loop(1, RESP, greet_row, 0)

    @pl.when(row > 0)
    def _():
        greet_row(0, 0)

    sources = (k_hbm, v_hbm, q_hbm, g_hbm)
    for i, source in enumerate(sources):
        pltpu.make_async_copy(source.at[0], x.at[i], in_sem.at[i]).start()

    length = len_ref[fst * (row - 1)]
    keep = jnp.where((row == 0) | (me < length), 1.0, 0.0).astype(jnp.float32)

    def columns(h):
        return pl.ds(pl.multiple_of(h * HEAD, HEAD), HEAD)

    def arrived(i):
        pltpu.make_async_copy(k_hbm.at[0], x.at[i], in_sem.at[i]).wait()

    def to_owner(p, s):
        return pltpu.make_async_remote_copy(
            src_ref=st.at[p, s], dst_ref=rc.at[p, me], send_sem=s1.at[p, s], recv_sem=r1.at[p, me],
            device_id=(s, row), device_id_type=MESH)

    def from_source(p, b):
        return pltpu.make_async_remote_copy(
            src_ref=st.at[p, b], dst_ref=rc.at[p, b], send_sem=s1.at[p, b], recv_sem=r1.at[p, b],
            device_id=(b, row), device_id_type=MESH)

    def to_source(p, b):
        return pltpu.make_async_remote_copy(
            src_ref=rt.at[p, b], dst_ref=fin.at[p, me], send_sem=s2.at[p, b], recv_sem=r2.at[p, me],
            device_id=(b, row), device_id_type=MESH)

    def from_owner(p, s):
        return pltpu.make_async_remote_copy(
            src_ref=rt.at[p, s], dst_ref=fin.at[p, s], send_sem=s2.at[p, s], recv_sem=r2.at[p, s],
            device_id=(s, row), device_id_type=MESH)

    def states(p):
        def one(j, _):
            h = ((me + 1) // 2 + j) % HEADS
            part = dot(x[2 * p, :, columns(h)], x[2 * p + 1, :, columns(h)], TN) * keep
            st[p, pl.ds(2 * h, 2)] = part.reshape(2, SHARD, HEAD)
            for half in range(2):
                @pl.when(2 * h + half != me)
                def _():
                    to_owner(p, 2 * h + half).start()
            return 0

        lax.fori_loop(0, HEADS, one, 0)
        rc[p, me] = st[p, me]

    def inside(h, _):
        c = columns(h)
        k0, k1 = x[0, :HALF, c], x[0, HALF:, c]
        v0, v1 = x[1, :HALF, c], x[1, HALF:, c]
        q0, q1 = x[2, :HALF, c], x[2, HALF:, c]
        g0, g1 = x[3, :HALF, c], x[3, HALF:, c]
        t = lax.broadcasted_iota(jnp.int32, (HALF, HALF), 0)
        s = lax.broadcasted_iota(jnp.int32, (HALF, HALF), 1)
        causal = t >= s

        def triangle(a0, a1, b0, b1):
            d0 = jnp.where(causal, dot(a0, b0, NT) * FACTOR, 0.0).astype(jnp.bfloat16)
            d1 = jnp.where(causal, dot(a1, b1, NT) * FACTOR, 0.0).astype(jnp.bfloat16)
            low = (dot(a1, b0, NT) * FACTOR).astype(jnp.bfloat16)
            return d0, low, d1

        a0, a10, a1 = triangle(q0, q1, k0, k1)
        p0, p10, p1 = triangle(g0, g1, v0, v1)
        intra[0, :HALF, c] = dot(a0, v0, NN)
        intra[0, HALF:, c] = dot(a10, v0, NN) + dot(a1, v1, NN)
        intra[1, :HALF, c] = dot(p0, k0, NN)
        intra[1, HALF:, c] = dot(p10, k0, NN) + dot(p1, k1, NN)
        intra[2, :HALF, c] = dot(a0, g0, TN) + dot(a10, g1, TN)
        intra[2, HALF:, c] = dot(a1, g1, TN)
        intra[3, :HALF, c] = dot(p0, q0, TN) + dot(p10, q1, TN)
        intra[3, HALF:, c] = dot(p1, q1, TN)
        return 0

    def gather_sources(p):
        def one(i, _):
            from_source(p, (me + i) % SEQ).wait_recv()
            return 0

        lax.fori_loop(1, SEQ, one, 0)

    def scanned(p, start):
        def one(i, total):
            b = p * (SEQ - 1) + (1 - 2 * p) * i
            rt[p, b] = total
            return total + rc[p, b]

        return lax.fori_loop(0, SEQ, one, start)

    def give_back(p):
        def one(i, _):
            to_source(p, (me + i) % SEQ).start()
            return 0

        lax.fori_loop(1, SEQ, one, 0)
        fin[p, me] = rt[p, me]

    def total_copy(to, slot):
        return pltpu.make_async_remote_copy(
            src_ref=zs, dst_ref=zr.at[slot], send_sem=sz.at[to], recv_sem=rz.at[slot],
            device_id=(me, to), device_id_type=MESH)

    def finish(p, h, first, second):
        for half in range(2):
            @pl.when(2 * h + half != me)
            def _():
                from_owner(p, 2 * h + half).wait_recv()
        c = columns(h)
        low = fin[p, pl.ds(2 * h, 2)].reshape(HEAD, HEAD).astype(jnp.bfloat16)
        o0, o1, i0, i1 = 2 * p, 2 * p + 1, 2 - 2 * p, 3 - 2 * p
        for o, i, ref, dims in ((o0, i0, first, NN), (o1, i1, second, NT)):
            ref[0, :, c] = ((intra[o, :, c] + FACTOR * dot(x[i, :, c], low, dims)) * keep).astype(jnp.bfloat16)

    def finish_all(p):
        def heads(p, first, second):
            def one(j, _):
                finish(p, ((me + SEQ - 1) // 2 + HEADS - j) % HEADS, first, second)
                return 0

            lax.fori_loop(0, HEADS, one, 0)

        @pl.when(p == 0)
        def _():
            heads(0, att_ref, gq_ref)

        @pl.when(p == 1)
        def _():
            heads(1, gv_ref, gk_ref)

    zero = jnp.zeros((SHARD, HEAD), jnp.float32)

    arrived(2 * fst)
    arrived(2 * fst + 1)

    @pl.when(row == 0)
    def _():
        pl.semaphore_wait(barrier, SEQ + RESP - 2)

    @pl.when(row > 0)
    def _():
        pl.semaphore_wait(barrier, SEQ)

    states(fst)
    arrived(2 * snd)
    arrived(2 * snd + 1)
    states(snd)
    lax.fori_loop(0, HEADS // 2, inside, 0)

    gather_sources(fst)
    zs[...] = scanned(fst, zero)

    @pl.when(row == 0)
    def _():
        def one(i, _):
            total_copy(i, 0).start()
            return 0

        lax.fori_loop(1, RESP, one, 0)

    @pl.when(row > 0)
    def _():
        pltpu.make_async_remote_copy(
            src_ref=zs, dst_ref=zr.at[row], send_sem=sz.at[0], recv_sem=rz.at[row],
            device_id=(me, 0), device_id_type=MESH).start()

    give_back(fst)
    lax.fori_loop(HEADS // 2, HEADS, inside, 0)

    gather_sources(snd)

    @pl.when(row == 0)
    def _():
        def one(i, _):
            total_copy(i, i).wait_recv()
            return 0

        lax.fori_loop(1, RESP, one, 0)
        scanned(snd, lax.fori_loop(1, RESP, lambda i, total: total + zr[i], zero))

    @pl.when(row > 0)
    def _():
        total_copy(0, 0).wait_recv()
        scanned(snd, zr[0])

    give_back(snd)
    finish_all(fst)
    finish_all(snd)

    def sent(i, _):
        for p in range(2):
            to_owner(p, (me + i) % SEQ).wait_send()
            to_source(p, (me + i) % SEQ).wait_send()
        return 0

    lax.fori_loop(1, SEQ, sent, 0)

    @pl.when(row == 0)
    def _():
        def one(i, _):
            total_copy(i, 0).wait_send()
            return 0

        lax.fori_loop(1, RESP, one, 0)

    @pl.when(row > 0)
    def _():
        total_copy(0, 0).wait_send()


def per_device(queries, keys, values, grad_out, lengths):
    shape = queries.shape
    pieces = pltpu.VMEM((2, SEQ, SHARD, HEAD), jnp.float32)
    attended, grad_queries, grad_values, grad_keys = pl.pallas_call(
        kernel,
        out_shape=[jax.ShapeDtypeStruct(shape, jnp.bfloat16)] * 4,
        in_specs=[pl.BlockSpec(memory_space=pltpu.SMEM)] + [pl.BlockSpec(memory_space=pltpu.HBM)] * 4,
        out_specs=[pl.BlockSpec(memory_space=pltpu.VMEM)] * 4,
        scratch_shapes=[
            pltpu.VMEM((4, *shape[1:]), jnp.bfloat16),
            pieces, pieces, pieces, pieces,
            pltpu.VMEM((SHARD, HEAD), jnp.float32),
            pltpu.VMEM((RESP, SHARD, HEAD), jnp.float32),
            pltpu.VMEM((4, *shape[1:]), jnp.float32),
            pltpu.SemaphoreType.DMA((4,)),
            pltpu.SemaphoreType.DMA((2, SEQ)),
            pltpu.SemaphoreType.DMA((2, SEQ)),
            pltpu.SemaphoreType.DMA((2, SEQ)),
            pltpu.SemaphoreType.DMA((2, SEQ)),
            pltpu.SemaphoreType.DMA((RESP,)),
            pltpu.SemaphoreType.DMA((RESP,)),
        ],
        compiler_params=pltpu.CompilerParams(
            collective_id=0, has_side_effects=True, vmem_limit_bytes=49 << 20),
        cost_estimate=pl.CostEstimate(flops=4 << 30, bytes_accessed=8 << 20, transcendentals=0),
        name="lightning",
    )(lengths, keys, values, queries, grad_out)
    return attended, grad_queries, grad_keys, grad_values


def solution(mesh):
    split = P("resp", "seq", None)
    return jax.shard_map(
        per_device,
        mesh=mesh,
        in_specs=(split, split, split, split, P()),
        out_specs=(split, split, split, split),
        check_vma=False,
    )
```

```python
import math

import jax
import jax.numpy as jnp
from jax import lax
from jax.experimental import pallas as pl
from jax.experimental.pallas import tpu as pltpu
from jax.sharding import PartitionSpec as P

HEADS = 8
HEAD = 128
BLOCK = 512
HALF = 256
SEQ = 16
RESP = 16
SHARD = HEADS * HEAD // SEQ
MESH = pl.DeviceIdType.MESH
FACTOR = 1.0 / math.sqrt(2.0 * SEQ * BLOCK)


def dot(a, b, dims):
    return lax.dot_general(a, b, (dims, ((), ())), preferred_element_type=jnp.float32)


NN = ((1,), (0,))
NT = ((1,), (1,))
TN = ((0,), (0,))


def kernel(
    len_ref, k_hbm, v_hbm, q_hbm, g_hbm,
    att_ref, gq_ref, gv_ref, gk_ref,
    x, st, rc, rt, fin, zs, zr, intra,
    in_sem, s1, r1, s2, r2, sz, rz,
):
    me = lax.axis_index("seq")
    row = lax.axis_index("resp")
    fst = (row + RESP - 2) // (RESP - 1)
    snd = 1 - fst

    barrier = pltpu.get_barrier_semaphore()

    def greet(i, _):
        pl.semaphore_signal(barrier, inc=1, device_id=((me + i) % SEQ, row), device_id_type=MESH)
        return 0

    lax.fori_loop(1, SEQ, greet, 0)

    def greet_row(i, _):
        pl.semaphore_signal(barrier, inc=1, device_id=(me, i), device_id_type=MESH)
        return 0

    @pl.when(row == 0)
    def _():
        lax.fori_loop(1, RESP, greet_row, 0)

    @pl.when(row > 0)
    def _():
        greet_row(0, 0)

    sources = (k_hbm, v_hbm, q_hbm, g_hbm)
    for i, source in enumerate(sources):
        pltpu.make_async_copy(source.at[0], x.at[i], in_sem.at[i]).start()

    length = len_ref[fst * (row - 1)]
    keep = jnp.where((row == 0) | (me < length), 1.0, 0.0).astype(jnp.float32)

    def columns(h):
        return pl.ds(pl.multiple_of(h * HEAD, HEAD), HEAD)

    def arrived(i):
        pltpu.make_async_copy(k_hbm.at[0], x.at[i], in_sem.at[i]).wait()

    def to_owner(p, s):
        return pltpu.make_async_remote_copy(
            src_ref=st.at[p, s], dst_ref=rc.at[p, me], send_sem=s1.at[p, s], recv_sem=r1.at[p, me],
            device_id=(s, row), device_id_type=MESH)

    def from_source(p, b):
        return pltpu.make_async_remote_copy(
            src_ref=st.at[p, b], dst_ref=rc.at[p, b], send_sem=s1.at[p, b], recv_sem=r1.at[p, b],
            device_id=(b, row), device_id_type=MESH)

    def to_source(p, b):
        return pltpu.make_async_remote_copy(
            src_ref=rt.at[p, b], dst_ref=fin.at[p, me], send_sem=s2.at[p, b], recv_sem=r2.at[p, me],
            device_id=(b, row), device_id_type=MESH)

    def from_owner(p, s):
        return pltpu.make_async_remote_copy(
            src_ref=rt.at[p, s], dst_ref=fin.at[p, s], send_sem=s2.at[p, s], recv_sem=r2.at[p, s],
            device_id=(s, row), device_id_type=MESH)

    def states(p):
        def one(j, _):
            h = ((me + 1) // 2 + j) % HEADS
            part = dot(x[2 * p, :, columns(h)], x[2 * p + 1, :, columns(h)], TN) * keep
            st[p, pl.ds(2 * h, 2)] = part.reshape(2, SHARD, HEAD)
            for half in range(2):
                @pl.when(2 * h + half != me)
                def _():
                    to_owner(p, 2 * h + half).start()
            return 0

        lax.fori_loop(0, HEADS, one, 0)
        rc[p, me] = st[p, me]

    def inside(h, _):
        c = columns(h)
        k0, k1 = x[0, :HALF, c], x[0, HALF:, c]
        v0, v1 = x[1, :HALF, c], x[1, HALF:, c]
        q0, q1 = x[2, :HALF, c], x[2, HALF:, c]
        g0, g1 = x[3, :HALF, c], x[3, HALF:, c]
        t = lax.broadcasted_iota(jnp.int32, (HALF, HALF), 0)
        s = lax.broadcasted_iota(jnp.int32, (HALF, HALF), 1)
        causal = t >= s

        def triangle(a0, a1, b0, b1):
            d0 = jnp.where(causal, dot(a0, b0, NT) * FACTOR, 0.0).astype(jnp.bfloat16)
            d1 = jnp.where(causal, dot(a1, b1, NT) * FACTOR, 0.0).astype(jnp.bfloat16)
            low = (dot(a1, b0, NT) * FACTOR).astype(jnp.bfloat16)
            return d0, low, d1

        a0, a10, a1 = triangle(q0, q1, k0, k1)
        p0, p10, p1 = triangle(g0, g1, v0, v1)
        intra[0, :HALF, c] = dot(a0, v0, NN)
        intra[0, HALF:, c] = dot(a10, v0, NN) + dot(a1, v1, NN)
        intra[1, :HALF, c] = dot(p0, k0, NN)
        intra[1, HALF:, c] = dot(p10, k0, NN) + dot(p1, k1, NN)
        intra[2, :HALF, c] = dot(a0, g0, TN) + dot(a10, g1, TN)
        intra[2, HALF:, c] = dot(a1, g1, TN)
        intra[3, :HALF, c] = dot(p0, q0, TN) + dot(p10, q1, TN)
        intra[3, HALF:, c] = dot(p1, q1, TN)
        return 0

    def gather_sources(p):
        def one(i, _):
            from_source(p, (me + i) % SEQ).wait_recv()
            return 0

        lax.fori_loop(1, SEQ, one, 0)

    def scanned(p, start):
        def one(i, total):
            b = p * (SEQ - 1) + (1 - 2 * p) * i
            rt[p, b] = total
            return total + rc[p, b]

        return lax.fori_loop(0, SEQ, one, start)

    def give_back(p):
        def one(i, _):
            to_source(p, (me + i) % SEQ).start()
            return 0

        lax.fori_loop(1, SEQ, one, 0)
        fin[p, me] = rt[p, me]

    def total_copy(to, slot):
        return pltpu.make_async_remote_copy(
            src_ref=zs, dst_ref=zr.at[slot], send_sem=sz.at[to], recv_sem=rz.at[slot],
            device_id=(me, to), device_id_type=MESH)

    def finish(p, h, first, second):
        for half in range(2):
            @pl.when(2 * h + half != me)
            def _():
                from_owner(p, 2 * h + half).wait_recv()
        c = columns(h)
        low = fin[p, pl.ds(2 * h, 2)].reshape(HEAD, HEAD).astype(jnp.bfloat16)
        o0, o1, i0, i1 = 2 * p, 2 * p + 1, 2 - 2 * p, 3 - 2 * p
        for o, i, ref, dims in ((o0, i0, first, NN), (o1, i1, second, NT)):
            ref[0, :, c] = ((intra[o, :, c] + FACTOR * dot(x[i, :, c], low, dims)) * keep).astype(jnp.bfloat16)

    def finish_all(p):
        def heads(p, first, second):
            def one(j, _):
                finish(p, ((me + SEQ - 1) // 2 + HEADS - j) % HEADS, first, second)
                return 0

            lax.fori_loop(0, HEADS, one, 0)

        @pl.when(p == 0)
        def _():
            heads(0, att_ref, gq_ref)

        @pl.when(p == 1)
        def _():
            heads(1, gv_ref, gk_ref)

    zero = jnp.zeros((SHARD, HEAD), jnp.float32)

    arrived(2 * fst)
    arrived(2 * fst + 1)

    @pl.when(row == 0)
    def _():
        pl.semaphore_wait(barrier, SEQ + RESP - 2)

    @pl.when(row > 0)
    def _():
        pl.semaphore_wait(barrier, SEQ)

    states(fst)
    arrived(2 * snd)
    arrived(2 * snd + 1)
    states(snd)
    lax.fori_loop(0, HEADS // 2, inside, 0)

    gather_sources(fst)
    zs[...] = scanned(fst, zero)

    @pl.when(row == 0)
    def _():
        def one(i, _):
            total_copy(i, 0).start()
            return 0

        lax.fori_loop(1, RESP, one, 0)

    @pl.when(row > 0)
    def _():
        pltpu.make_async_remote_copy(
            src_ref=zs, dst_ref=zr.at[row], send_sem=sz.at[0], recv_sem=rz.at[row],
            device_id=(me, 0), device_id_type=MESH).start()

    give_back(fst)
    lax.fori_loop(HEADS // 2, HEADS, inside, 0)

    gather_sources(snd)

    @pl.when(row == 0)
    def _():
        def one(i, _):
            total_copy(i, i).wait_recv()
            return 0

        lax.fori_loop(1, RESP, one, 0)
        scanned(snd, lax.fori_loop(1, RESP, lambda i, total: total + zr[i], zero))

    @pl.when(row > 0)
    def _():
        total_copy(0, 0).wait_recv()
        scanned(snd, zr[0])

    give_back(snd)
    finish_all(fst)
    finish_all(snd)

    def sent(i, _):
        for p in range(2):
            to_owner(p, (me + i) % SEQ).wait_send()
            to_source(p, (me + i) % SEQ).wait_send()
        return 0

    lax.fori_loop(1, SEQ, sent, 0)

    @pl.when(row == 0)
    def _():
        def one(i, _):
            total_copy(i, 0).wait_send()
            return 0

        lax.fori_loop(1, RESP, one, 0)

    @pl.when(row > 0)
    def _():
        total_copy(0, 0).wait_send()


def write_out(*refs):
    copies = [pltpu.make_async_copy(refs[i], refs[4 + i], refs[8].at[i]) for i in range(4)]
    for copy in copies:
        copy.start()
    for copy in copies:
        copy.wait()


def written(*arrays):
    return pl.pallas_call(
        write_out,
        out_shape=[jax.ShapeDtypeStruct(a.shape, a.dtype) for a in arrays],
        in_specs=[pl.BlockSpec(memory_space=pltpu.VMEM)] * 4,
        out_specs=[pl.BlockSpec(memory_space=pl.ANY)] * 4,
        scratch_shapes=[pltpu.SemaphoreType.DMA((4,))],
        compiler_params=pltpu.CompilerParams(vmem_limit_bytes=1 << 20),
        name="write_out",
    )(*arrays)


def per_device(queries, keys, values, grad_out, lengths):
    shape = queries.shape
    pieces = pltpu.VMEM((2, SEQ, SHARD, HEAD), jnp.float32)
    attended, grad_queries, grad_values, grad_keys = pl.pallas_call(
        kernel,
        out_shape=[jax.ShapeDtypeStruct(shape, jnp.bfloat16)] * 4,
        in_specs=[pl.BlockSpec(memory_space=pltpu.SMEM)] + [pl.BlockSpec(memory_space=pltpu.HBM)] * 4,
        out_specs=[pl.BlockSpec(memory_space=pltpu.VMEM)] * 4,
        scratch_shapes=[
            pltpu.VMEM((4, *shape[1:]), jnp.bfloat16),
            pieces, pieces, pieces, pieces,
            pltpu.VMEM((SHARD, HEAD), jnp.float32),
            pltpu.VMEM((RESP, SHARD, HEAD), jnp.float32),
            pltpu.VMEM((4, *shape[1:]), jnp.float32),
            pltpu.SemaphoreType.DMA((4,)),
            pltpu.SemaphoreType.DMA((2, SEQ)),
            pltpu.SemaphoreType.DMA((2, SEQ)),
            pltpu.SemaphoreType.DMA((2, SEQ)),
            pltpu.SemaphoreType.DMA((2, SEQ)),
            pltpu.SemaphoreType.DMA((RESP,)),
            pltpu.SemaphoreType.DMA((RESP,)),
        ],
        compiler_params=pltpu.CompilerParams(
            collective_id=0, has_side_effects=True, vmem_limit_bytes=49 << 20),
        cost_estimate=pl.CostEstimate(flops=4 << 30, bytes_accessed=8 << 20, transcendentals=0),
        name="lightning",
    )(lengths, keys, values, queries, grad_out)
    return written(attended, grad_queries, grad_keys, grad_values)


def solution(mesh):
    split = P("resp", "seq", None)
    return jax.shard_map(
        per_device,
        mesh=mesh,
        in_specs=(split, split, split, split, P()),
        out_specs=(split, split, split, split),
        check_vma=False,
    )
```

```python
import math

import jax
import jax.numpy as jnp
from jax import lax
from jax.experimental import pallas as pl
from jax.experimental.pallas import tpu as pltpu
from jax.sharding import PartitionSpec as P

HEADS = 8
HEAD = 128
BLOCK = 512
HALF = 256
SEQ = 16
RESP = 16
SHARD = HEADS * HEAD // SEQ
MESH = pl.DeviceIdType.MESH
FACTOR = 1.0 / math.sqrt(2.0 * SEQ * BLOCK)


def dot(a, b, dims):
    return lax.dot_general(a, b, (dims, ((), ())), preferred_element_type=jnp.float32)


NN = ((1,), (0,))
NT = ((1,), (1,))
TN = ((0,), (0,))


def kernel(
    len_ref, k_hbm, v_hbm, q_hbm, g_hbm,
    att_ref, gq_ref, gv_ref, gk_ref,
    x, st, rc, rt, fin, zs, zr, intra,
    in_sem, s1, r1, s2, r2, sz, rz,
):
    me = lax.axis_index("seq")
    row = lax.axis_index("resp")
    fst = (row + RESP - 2) // (RESP - 1)
    snd = 1 - fst

    barrier = pltpu.get_barrier_semaphore()

    def greet(i, _):
        pl.semaphore_signal(barrier, inc=1, device_id=((me + i) % SEQ, row), device_id_type=MESH)
        return 0

    lax.fori_loop(1, SEQ, greet, 0)

    def greet_row(i, _):
        pl.semaphore_signal(barrier, inc=1, device_id=(me, i), device_id_type=MESH)
        return 0

    @pl.when(row == 0)
    def _():
        lax.fori_loop(1, RESP, greet_row, 0)

    @pl.when(row > 0)
    def _():
        greet_row(0, 0)

    sources = (k_hbm, v_hbm, q_hbm, g_hbm)
    for i, source in enumerate(sources):
        pltpu.make_async_copy(source.at[0], x.at[i], in_sem.at[i]).start()

    length = len_ref[fst * (row - 1)]
    keep = jnp.where((row == 0) | (me < length), 1.0, 0.0).astype(jnp.float32)

    def columns(h):
        return pl.ds(pl.multiple_of(h * HEAD, HEAD), HEAD)

    def arrived(i):
        pltpu.make_async_copy(k_hbm.at[0], x.at[i], in_sem.at[i]).wait()

    def to_owner(p, s):
        return pltpu.make_async_remote_copy(
            src_ref=st.at[p, s], dst_ref=rc.at[p, me], send_sem=s1.at[p, s], recv_sem=r1.at[p, me],
            device_id=(s, row), device_id_type=MESH)

    def from_source(p, b):
        return pltpu.make_async_remote_copy(
            src_ref=st.at[p, b], dst_ref=rc.at[p, b], send_sem=s1.at[p, b], recv_sem=r1.at[p, b],
            device_id=(b, row), device_id_type=MESH)

    def to_source(p, b):
        return pltpu.make_async_remote_copy(
            src_ref=rt.at[p, b], dst_ref=fin.at[p, me], send_sem=s2.at[p, b], recv_sem=r2.at[p, me],
            device_id=(b, row), device_id_type=MESH)

    def from_owner(p, s):
        return pltpu.make_async_remote_copy(
            src_ref=rt.at[p, s], dst_ref=fin.at[p, s], send_sem=s2.at[p, s], recv_sem=r2.at[p, s],
            device_id=(s, row), device_id_type=MESH)

    def states(p):
        def one(j, _):
            h = ((me + 1) // 2 + j) % HEADS
            part = dot(x[2 * p, :, columns(h)], x[2 * p + 1, :, columns(h)], TN) * keep
            st[p, pl.ds(2 * h, 2)] = part.reshape(2, SHARD, HEAD)
            return 0

        lax.fori_loop(0, HEADS, one, 0, unroll=4)

    def give_out(p):
        def one(i, _):
            to_owner(p, (me + i) % SEQ).start()
            return 0

        lax.fori_loop(1, SEQ, one, 0)
        rc[p, me] = st[p, me]

    def inside(h, _):
        c = columns(h)
        k0, k1 = x[0, :HALF, c], x[0, HALF:, c]
        v0, v1 = x[1, :HALF, c], x[1, HALF:, c]
        q0, q1 = x[2, :HALF, c], x[2, HALF:, c]
        g0, g1 = x[3, :HALF, c], x[3, HALF:, c]
        t = lax.broadcasted_iota(jnp.int32, (HALF, HALF), 0)
        s = lax.broadcasted_iota(jnp.int32, (HALF, HALF), 1)
        causal = t >= s

        def triangle(a0, a1, b0, b1):
            d0 = jnp.where(causal, dot(a0, b0, NT) * FACTOR, 0.0).astype(jnp.bfloat16)
            d1 = jnp.where(causal, dot(a1, b1, NT) * FACTOR, 0.0).astype(jnp.bfloat16)
            low = (dot(a1, b0, NT) * FACTOR).astype(jnp.bfloat16)
            return d0, low, d1

        a0, a10, a1 = triangle(q0, q1, k0, k1)
        p0, p10, p1 = triangle(g0, g1, v0, v1)
        intra[0, :HALF, c] = dot(a0, v0, NN)
        intra[0, HALF:, c] = dot(a10, v0, NN) + dot(a1, v1, NN)
        intra[1, :HALF, c] = dot(p0, k0, NN)
        intra[1, HALF:, c] = dot(p10, k0, NN) + dot(p1, k1, NN)
        intra[2, :HALF, c] = dot(a0, g0, TN) + dot(a10, g1, TN)
        intra[2, HALF:, c] = dot(a1, g1, TN)
        intra[3, :HALF, c] = dot(p0, q0, TN) + dot(p10, q1, TN)
        intra[3, HALF:, c] = dot(p1, q1, TN)
        return 0

    def gather_sources(p):
        def one(i, _):
            from_source(p, (me + i) % SEQ).wait_recv()
            return 0

        lax.fori_loop(1, SEQ, one, 0)

    def scanned(p, start):
        def one(i, total):
            b = p * (SEQ - 1) + (1 - 2 * p) * i
            rt[p, b] = total
            return total + rc[p, b]

        return lax.fori_loop(0, SEQ, one, start)

    def give_back(p):
        def one(i, _):
            to_source(p, (me + i) % SEQ).start()
            return 0

        lax.fori_loop(1, SEQ, one, 0)
        fin[p, me] = rt[p, me]

    def total_copy(to, slot):
        return pltpu.make_async_remote_copy(
            src_ref=zs, dst_ref=zr.at[slot], send_sem=sz.at[to], recv_sem=rz.at[slot],
            device_id=(me, to), device_id_type=MESH)

    def finish(p, h, first, second):
        for half in range(2):
            @pl.when(2 * h + half != me)
            def _():
                from_owner(p, 2 * h + half).wait_recv()
        c = columns(h)
        low = fin[p, pl.ds(2 * h, 2)].reshape(HEAD, HEAD).astype(jnp.bfloat16)
        o0, o1, i0, i1 = 2 * p, 2 * p + 1, 2 - 2 * p, 3 - 2 * p
        for o, i, ref, dims in ((o0, i0, first, NN), (o1, i1, second, NT)):
            ref[0, :, c] = ((intra[o, :, c] + FACTOR * dot(x[i, :, c], low, dims)) * keep).astype(jnp.bfloat16)

    def finish_all(p):
        def heads(p, first, second):
            def one(j, _):
                finish(p, ((me + SEQ - 1) // 2 + HEADS - j) % HEADS, first, second)
                return 0

            lax.fori_loop(0, HEADS, one, 0, unroll=2)

        @pl.when(p == 0)
        def _():
            heads(0, att_ref, gq_ref)

        @pl.when(p == 1)
        def _():
            heads(1, gv_ref, gk_ref)

    zero = jnp.zeros((SHARD, HEAD), jnp.float32)

    arrived(2 * fst)
    arrived(2 * fst + 1)

    states(fst)

    @pl.when(row == 0)
    def _():
        pl.semaphore_wait(barrier, SEQ + RESP - 2)

    @pl.when(row > 0)
    def _():
        pl.semaphore_wait(barrier, SEQ)

    give_out(fst)
    arrived(2 * snd)
    arrived(2 * snd + 1)
    states(snd)
    give_out(snd)
    lax.fori_loop(0, HEADS // 2, inside, 0)

    gather_sources(fst)
    zs[...] = scanned(fst, zero)

    @pl.when(row == 0)
    def _():
        def one(i, _):
            total_copy(i, 0).start()
            return 0

        lax.fori_loop(1, RESP, one, 0)

    @pl.when(row > 0)
    def _():
        pltpu.make_async_remote_copy(
            src_ref=zs, dst_ref=zr.at[row], send_sem=sz.at[0], recv_sem=rz.at[row],
            device_id=(me, 0), device_id_type=MESH).start()

    give_back(fst)
    lax.fori_loop(HEADS // 2, HEADS, inside, 0)

    gather_sources(snd)

    @pl.when(row == 0)
    def _():
        def one(i, _):
            total_copy(i, i).wait_recv()
            return 0

        lax.fori_loop(1, RESP, one, 0)
        scanned(snd, lax.fori_loop(1, RESP, lambda i, total: total + zr[i], zero))

    @pl.when(row > 0)
    def _():
        total_copy(0, 0).wait_recv()
        scanned(snd, zr[0])

    give_back(snd)
    finish_all(fst)
    finish_all(snd)

    def sent(i, _):
        for p in range(2):
            to_owner(p, (me + i) % SEQ).wait_send()
            to_source(p, (me + i) % SEQ).wait_send()
        return 0

    lax.fori_loop(1, SEQ, sent, 0)

    @pl.when(row == 0)
    def _():
        def one(i, _):
            total_copy(i, 0).wait_send()
            return 0

        lax.fori_loop(1, RESP, one, 0)

    @pl.when(row > 0)
    def _():
        total_copy(0, 0).wait_send()


def write_out(*refs):
    copies = [pltpu.make_async_copy(refs[i], refs[4 + i], refs[8].at[i]) for i in range(4)]
    for copy in copies:
        copy.start()
    for copy in copies:
        copy.wait()


def written(*arrays):
    return pl.pallas_call(
        write_out,
        out_shape=[jax.ShapeDtypeStruct(a.shape, a.dtype) for a in arrays],
        in_specs=[pl.BlockSpec(memory_space=pltpu.VMEM)] * 4,
        out_specs=[pl.BlockSpec(memory_space=pl.ANY)] * 4,
        scratch_shapes=[pltpu.SemaphoreType.DMA((4,))],
        compiler_params=pltpu.CompilerParams(vmem_limit_bytes=1 << 20),
        name="write_out",
    )(*arrays)


def per_device(queries, keys, values, grad_out, lengths):
    shape = queries.shape
    pieces = pltpu.VMEM((2, SEQ, SHARD, HEAD), jnp.float32)
    attended, grad_queries, grad_values, grad_keys = pl.pallas_call(
        kernel,
        out_shape=[jax.ShapeDtypeStruct(shape, jnp.bfloat16)] * 4,
        in_specs=[pl.BlockSpec(memory_space=pltpu.SMEM)] + [pl.BlockSpec(memory_space=pltpu.HBM)] * 4,
        out_specs=[pl.BlockSpec(memory_space=pltpu.VMEM)] * 4,
        scratch_shapes=[
            pltpu.VMEM((4, *shape[1:]), jnp.bfloat16),
            pieces, pieces, pieces, pieces,
            pltpu.VMEM((SHARD, HEAD), jnp.float32),
            pltpu.VMEM((RESP, SHARD, HEAD), jnp.float32),
            pltpu.VMEM((4, *shape[1:]), jnp.float32),
            pltpu.SemaphoreType.DMA((4,)),
            pltpu.SemaphoreType.DMA((2, SEQ)),
            pltpu.SemaphoreType.DMA((2, SEQ)),
            pltpu.SemaphoreType.DMA((2, SEQ)),
            pltpu.SemaphoreType.DMA((2, SEQ)),
            pltpu.SemaphoreType.DMA((RESP,)),
            pltpu.SemaphoreType.DMA((RESP,)),
        ],
        compiler_params=pltpu.CompilerParams(
            collective_id=0, has_side_effects=True, vmem_limit_bytes=49 << 20),
        cost_estimate=pl.CostEstimate(flops=4 << 30, bytes_accessed=8 << 20, transcendentals=0),
        name="lightning",
    )(lengths, keys, values, queries, grad_out)
    return written(attended, grad_queries, grad_keys, grad_values)


def solution(mesh):
    split = P("resp", "seq", None)
    return jax.shard_map(
        per_device,
        mesh=mesh,
        in_specs=(split, split, split, split, P()),
        out_specs=(split, split, split, split),
        check_vma=False,
    )
```
